32 devices in a mesh: dp: 8 (over y, x, core), fsdp: 4 (over z).
Axes of the slice: x: 2, y: 2, z: 4, core: 2. Of those that a mesh axis runs over, the one named last changes fastest.
Arguments:
- inputs: float32 [4096, 1024], P(('dp', 'fsdp')), may hold values from -6 to 6
- cotangent: float32 [4096, 1024], P(('dp', 'fsdp')), may hold values from -6 to 6
- starts: int32 [64], P('dp'), may hold values from 0 to 1, as said below
- filled: int32 [64], P('dp'), may hold values from 1 to 64, as said below
- norm_gain: bfloat16 [1024], P('dp'), may hold values from 0.5 to 1.5
- query_weight: bfloat16 [1024, 512], P('dp', 'fsdp'), may hold values from -0.1875 to 0.1875
- key_weight: bfloat16 [1024, 512], P('dp', 'fsdp'), may hold values from -0.1875 to 0.1875
- value_weight: bfloat16 [1024, 1024], P('dp', 'fsdp'), may hold values from -0.1875 to 0.1875
- decay_weight: bfloat16 [1024, 4], P('dp', 'fsdp'), may hold values from -0.1875 to 0.1875
- beta_weight: bfloat16 [1024, 4], P('dp', 'fsdp'), may hold values from -0.1875 to 0.1875
- gating_weight: bfloat16 [1024, 1024], P('dp', 'fsdp'), may hold values from -0.1875 to 0.1875
- output_weight: bfloat16 [1024, 1024], P('fsdp', 'dp'), may hold values from -0.375 to 0.375
- second_gain: bfloat16 [1024], P('dp'), may hold values from 0.5 to 1.5
- gate_weight: bfloat16 [1024, 2816], P('dp', 'fsdp'), may hold values from -0.1875 to 0.1875
- up_weight: bfloat16 [1024, 2816], P('dp', 'fsdp'), may hold values from -0.1875 to 0.1875
- down_weight: bfloat16 [2816, 1024], P('fsdp', 'dp'), may hold values from -0.109375 to 0.109375
- conv_query: float32 [4, 512], P(None, 'fsdp'), may hold values from -3 to 3
- conv_key: float32 [4, 512], P(None, 'fsdp'), may hold values from -3 to 3
- conv_value: float32 [4, 1024], P(None, 'fsdp'), may hold values from -3 to 3
- decay_log: float32 [4], P('fsdp'), may hold values from -4 to 0
- decay_bias: float32 [4], P('fsdp'), may hold values from -4 to -1
- head_gain: float32 [256], replicated, may hold values from 0.5 to 1.5
Outputs:
- outputs: float32 [4096, 1024], P(('dp', 'fsdp'))
- inputs_gradient: float32 [4096, 1024], P(('dp', 'fsdp'))
- norm_gain_gradient: float32 [1024], replicated
- query_gradient: float32 [1024, 512], P('dp', 'fsdp')
- key_gradient: float32 [1024, 512], P('dp', 'fsdp')
- value_gradient: float32 [1024, 1024], P('dp', 'fsdp')
- decay_gradient: float32 [1024, 4], P('dp', 'fsdp')
- beta_gradient: float32 [1024, 4], P('dp', 'fsdp')
- gating_gradient: float32 [1024, 1024], P('dp', 'fsdp')
- output_gradient: float32 [1024, 1024], P('fsdp', 'dp')
- second_gain_gradient: float32 [1024], replicated
- gate_gradient: float32 [1024, 2816], P('dp', 'fsdp')
- up_gradient: float32 [1024, 2816], P('dp', 'fsdp')
- down_gradient: float32 [2816, 1024], P('fsdp', 'dp')
- conv_query_gradient: float32 [4, 512], P(None, 'fsdp')
- conv_key_gradient: float32 [4, 512], P(None, 'fsdp')
- conv_value_gradient: float32 [4, 1024], P(None, 'fsdp')
- decay_log_gradient: float32 [4], P('fsdp')
- decay_bias_gradient: float32 [4], P('fsdp')
- head_gain_gradient: float32 [256], replicated
The draws below stay inside these ranges and needn't reach their ends.
Inputs may be any that keep to these rules, and one draw needn't show every extreme that they name: `starts`: the first span of each aligned group of 512 rows begins a sequence. `filled`: 64 in every span whose next span continues its sequence.
All inputs are finite; a program needn't handle non-finite values.
Results may differ from the reference program's by a relative error of at most 0.017.
Values may be sent and summed in bfloat16 or wider, within the bound.
A program may use at most 128 MiB of HBM per device.

```python
import math
from functools import partial
import jax
import jax.numpy as jnp
from jax import lax

D = 1024
HEADS = 4
DK = 128
DV = 256
FF = 2816
CONV = 4
SPAN = 64
TOK_DEV = 128
TOKENS = 4096
N_FSDP = 4
DEVICES = 32


def plan_spans(key):
    per_group = N_FSDP * TOK_DEV // SPAN
    count = TOKENS // SPAN
    index = jnp.arange(count, dtype=jnp.int32)
    flags = jax.random.randint(jax.random.fold_in(key, 11), (count,), 0, 2, dtype=jnp.int32)
    flags = jnp.where(index % per_group == 0, 1, flags)
    flags = jnp.where(index == 1, 0, flags)
    ending = jnp.concatenate([flags[1:], jnp.ones((1,), jnp.int32)])
    lengths = jax.random.randint(jax.random.fold_in(key, 12), (count,), 1, SPAN + 1, dtype=jnp.int32)
    lengths = jnp.where(ending == 1, lengths, SPAN)
    return (flags.astype(jnp.int32), lengths.astype(jnp.int32))


def draw_starts(key, part):
    return plan_spans(key)[0]


def draw_filled(key, part):
    return plan_spans(key)[1]


def block_scale(rng, extent, cuts, smallest, high):
    def one(dim, shards_of):
        steps = jax.random.uniform(jax.random.fold_in(jax.random.fold_in(rng, 6), dim), (shards_of,), jnp.float32, smallest / len(cuts), high / len(cuts))
        return jnp.repeat(jnp.exp(steps), extent[dim] // shards_of).reshape((-1,) + (1,) * (len(extent) - dim - 1))

    level = one(*cuts[0])
    for cut in cuts[1:]:
        level = level * one(*cut)
    return level


def scatter_about(key, extent, scale, bound, split=(), kind=jnp.bfloat16):
    entries = scale * jax.random.normal(key, extent, jnp.float32)
    if split:
        entries = entries * block_scale(key, extent, split, -0.22, 0.18)
    return jnp.clip(entries, -bound, bound).astype(kind)


def setup_inputs(seed: int = 0) -> dict:
    key_list = jax.random.split(jax.random.key(seed), 23)
    inputs = scatter_about(key_list[0], (TOKENS, D), 1.0, 6.0, ((0, 32),), jnp.float32)
    cotangent = scatter_about(key_list[1], (TOKENS, D), 1.0, 6.0, ((0, 32),), jnp.float32)
    starts = draw_starts(jax.random.fold_in(key_list[22], 71), 0)
    filled = draw_filled(jax.random.fold_in(key_list[22], 71), 0)
    norm_gain = jnp.clip(1.0 + 0.1 * jax.random.normal(key_list[4], (D,), jnp.float32), 0.5, 1.5).astype(jnp.bfloat16)
    query_weight = scatter_about(key_list[5], (D, HEADS * DK), D ** -0.5, 0.1875, ((0, 8), (1, 4)))
    key_weight = scatter_about(key_list[6], (D, HEADS * DK), D ** -0.5, 0.1875, ((0, 8), (1, 4)))
    value_weight = scatter_about(key_list[7], (D, HEADS * DV), D ** -0.5, 0.1875, ((0, 8), (1, 4)))
    decay_weight = scatter_about(key_list[8], (D, HEADS), D ** -0.5, 0.1875, ((0, 8), (1, 4)))
    beta_weight = scatter_about(key_list[9], (D, HEADS), D ** -0.5, 0.1875, ((0, 8), (1, 4)))
    gating_weight = scatter_about(key_list[10], (D, HEADS * DV), D ** -0.5, 0.1875, ((0, 8), (1, 4)))
    output_weight = scatter_about(key_list[11], (HEADS * DV, D), (HEADS * DV // 4) ** -0.5, 0.375, ((0, 4), (1, 8)))
    second_gain = jnp.clip(1.0 + 0.1 * jax.random.normal(key_list[12], (D,), jnp.float32), 0.5, 1.5).astype(jnp.bfloat16)
    gate_weight = scatter_about(key_list[13], (D, FF), D ** -0.5, 0.1875, ((0, 8), (1, 4)))
    up_weight = scatter_about(key_list[14], (D, FF), D ** -0.5, 0.1875, ((0, 8), (1, 4)))
    down_weight = scatter_about(key_list[15], (FF, D), FF ** -0.5, 0.109375, ((0, 4), (1, 8)))
    conv_query = scatter_about(key_list[16], (CONV, HEADS * DK), 0.5, 3.0, ((1, 4),), jnp.float32)
    conv_key = scatter_about(key_list[17], (CONV, HEADS * DK), 0.5, 3.0, ((1, 4),), jnp.float32)
    conv_value = scatter_about(key_list[18], (CONV, HEADS * DV), 0.5, 3.0, ((1, 4),), jnp.float32)
    decay_log = jnp.clip(-4.0 + 4.0 * jax.random.uniform(key_list[19], (HEADS,), jnp.float32) ** block_scale(key_list[19], (HEADS,), ((0, 4),), -0.2, 0.2), -4.0, 0.0)
    decay_bias = jnp.clip(-4.0 + 3.0 * jax.random.uniform(key_list[20], (HEADS,), jnp.float32) ** block_scale(key_list[20], (HEADS,), ((0, 4),), -0.2, 0.2), -4.0, -1.0)
    head_gain = jnp.clip(1.0 + 0.1 * jax.random.normal(key_list[21], (DV,), jnp.float32), 0.5, 1.5)
    return dict(inputs=inputs, cotangent=cotangent, starts=starts, filled=filled, norm_gain=norm_gain, query_weight=query_weight, key_weight=key_weight, value_weight=value_weight, decay_weight=decay_weight, beta_weight=beta_weight, gating_weight=gating_weight, output_weight=output_weight, second_gain=second_gain, gate_weight=gate_weight, up_weight=up_weight, down_weight=down_weight, conv_query=conv_query, conv_key=conv_key, conv_value=conv_value, decay_log=decay_log, decay_bias=decay_bias, head_gain=head_gain)


EPS = 1e-06
HIGH = lax.Precision.HIGHEST

def norm_rows(values, gain):
    return values * lax.rsqrt(lax.optimization_barrier(jnp.mean(values * values, axis=-1, keepdims=True)) + EPS) * gain

def unit_heads(values):
    return values * lax.rsqrt(lax.optimization_barrier(jnp.sum(values * values, axis=-1, keepdims=True)) + EPS)

def lead_dot(left, right):
    return lax.dot_general(left.astype(jnp.float32), right.astype(jnp.float32), (((0,), (0,)), ((), ())), preferred_element_type=jnp.float32)

def tail_dot(left, right):
    return lax.dot_general(left.astype(jnp.float32), right.astype(jnp.float32), (((1,), (1,)), ((), ())), preferred_element_type=jnp.float32)

def short_conv(values, taps, same):
    total = values * taps[0]
    for back in range(1, taps.shape[0]):
        moved = jnp.concatenate([jnp.zeros((back, values.shape[1]), values.dtype), values[:-back]], axis=0)
        total = total + moved * taps[back] * same[back]
    return jax.nn.silu(total)

def token_masks(starts, filled, taps):
    count = starts.shape[0]
    seq_ids = jnp.repeat(jnp.cumsum(starts, dtype=jnp.int32), SPAN)
    within = jnp.arange(count * SPAN, dtype=jnp.int32) % SPAN
    valid = (within < jnp.repeat(filled, SPAN)).astype(jnp.float32)[:, None]
    same = [jnp.ones_like(valid)]
    for back in range(1, taps):
        earlier = jnp.concatenate([jnp.full((back,), -1, jnp.int32), seq_ids[:-back]])
        same.append((earlier == seq_ids).astype(jnp.float32)[:, None])
    return (same, starts.astype(jnp.float32), valid)

def span_step(state, block):
    query, key, value, beta, decay, start = block
    state = state * (1.0 - start)
    size = decay.shape[-1]
    rows = lax.broadcasted_iota(jnp.int32, (size, size), 0)
    cols = lax.broadcasted_iota(jnp.int32, (size, size), 1)
    inside = rows >= cols
    strict = (rows > cols).astype(decay.dtype)
    total = jnp.cumsum(decay, axis=-1)
    spread = total[:, :, None] - total[:, None, :]
    factor = jnp.exp(jnp.where(inside, spread, 0.0)) * inside.astype(decay.dtype)
    intersection = jnp.einsum('hid,hjd->hij', key, key, precision=HIGH)
    system = jnp.eye(size, dtype=decay.dtype) + beta[:, :, None] * intersection * factor * strict
    scaled = (beta * jnp.exp(total))[:, :, None] * key
    solved_keys = jax.scipy.linalg.solve_triangular(system, scaled, lower=True, unit_diagonal=True)
    solved_values = jax.scipy.linalg.solve_triangular(system, beta[:, :, None] * value, lower=True, unit_diagonal=True)
    fresh = solved_values - jnp.einsum('hcd,hde->hce', solved_keys, state, precision=HIGH)
    scores = jnp.einsum('hid,hjd->hij', query, key, precision=HIGH) * factor
    result = jnp.einsum('hcd,hde->hce', query * jnp.exp(total)[:, :, None], state, precision=HIGH)
    result = result + jnp.einsum('hij,hje->hie', scores, fresh, precision=HIGH)
    final = total[:, -1:]
    carried = key * jnp.exp(final - total)[:, :, None]
    state = jnp.exp(final)[:, :, None] * state + jnp.einsum('hjd,hje->hde', carried, fresh, precision=HIGH)
    return (state, result)

def delta_rule(query, key, value, beta, decay, starts):
    count = starts.shape[0]

    def blocks(values):
        shaped = values.reshape((count, values.shape[0] // count) + values.shape[1:])
        return jnp.swapaxes(shaped, 1, 2)
    initial = jnp.zeros((query.shape[1], query.shape[2], value.shape[2]), query.dtype)
    _, result = lax.scan(span_step, initial, (blocks(query), blocks(key), blocks(value), blocks(beta), blocks(decay), starts))
    return jnp.swapaxes(result, 1, 2).reshape(value.shape)

def mixer(same, starts, valid, query_pre, key_pre, value_pre, decay_pre, beta_pre, gating_pre, conv_query, conv_key, conv_value, decay_log, decay_bias, head_gain):
    count = query_pre.shape[0]
    query = unit_heads(short_conv(query_pre, conv_query, same).reshape(count, HEADS, DK)) * DK ** (-0.5)
    key = unit_heads(short_conv(key_pre, conv_key, same).reshape(count, HEADS, DK))
    value = short_conv(value_pre, conv_value, same).reshape(count, HEADS, DV)
    beta = jax.nn.sigmoid(beta_pre)
    decay = -jnp.exp(decay_log) * jax.nn.softplus(decay_pre + decay_bias)
    attended = delta_rule(query, key, value, beta, decay, starts)
    normal = attended * lax.rsqrt(lax.optimization_barrier(jnp.mean(attended * attended, axis=-1, keepdims=True)) + EPS) * head_gain
    gated = normal * jax.nn.silu(gating_pre.reshape(count, HEADS, DV)) * valid[:, :, None]
    return gated.reshape(count, HEADS * DV)

def forward(inputs, masks, mats, smalls):
    norm_gain, query_weight, key_weight, value_weight, decay_weight, beta_weight, gating_weight, output_weight, second_gain, gate_weight, up_weight, down_weight = mats
    same, starts, valid = masks
    normed = norm_rows(inputs, norm_gain.astype(jnp.float32)).astype(jnp.bfloat16)
    q_in = jnp.dot(normed.astype(jnp.float32), query_weight.astype(jnp.float32), preferred_element_type=jnp.float32)
    k_in = jnp.dot(normed.astype(jnp.float32), key_weight.astype(jnp.float32), preferred_element_type=jnp.float32)
    v_in = jnp.dot(normed.astype(jnp.float32), value_weight.astype(jnp.float32), preferred_element_type=jnp.float32)
    d_in = jnp.dot(normed.astype(jnp.float32), decay_weight.astype(jnp.float32), preferred_element_type=jnp.float32)
    b_in = jnp.dot(normed.astype(jnp.float32), beta_weight.astype(jnp.float32), preferred_element_type=jnp.float32)
    g_in = jnp.dot(normed.astype(jnp.float32), gating_weight.astype(jnp.float32), preferred_element_type=jnp.float32)
    conv_query, conv_key, conv_value, decay_log, decay_bias, head_gain = smalls
    mixed, mixer_back = jax.vjp(partial(mixer, same, starts, valid), q_in, k_in, v_in, d_in, b_in, g_in, conv_query, conv_key, conv_value, decay_log, decay_bias, head_gain)
    mixed_bf = mixed.astype(jnp.bfloat16)
    hidden = inputs + jnp.dot(mixed_bf.astype(jnp.float32), output_weight.astype(jnp.float32), preferred_element_type=jnp.float32)
    second = norm_rows(hidden, second_gain.astype(jnp.float32)).astype(jnp.bfloat16)
    gate = jnp.dot(second.astype(jnp.float32), gate_weight.astype(jnp.float32), preferred_element_type=jnp.float32)
    upper = jnp.dot(second.astype(jnp.float32), up_weight.astype(jnp.float32), preferred_element_type=jnp.float32)
    acted = (jax.nn.silu(gate) * upper).astype(jnp.bfloat16)
    outputs = hidden + jnp.dot(acted.astype(jnp.float32), down_weight.astype(jnp.float32), preferred_element_type=jnp.float32)
    return (outputs, (normed, mixed_bf, mixer_back, hidden, second, gate, upper, acted))

def backward_top(cotangent, saved, mats):
    normed, mixed_bf, mixer_back, hidden, second, gate, upper, acted = saved
    second_gain, gate_weight, up_weight, down_weight = (mats[8], mats[9], mats[10], mats[11])
    cot_bf = cotangent.astype(jnp.bfloat16)
    down_grad = lead_dot(acted, cot_bf)
    acted_back = tail_dot(cot_bf, down_weight)
    sigma = jax.nn.sigmoid(gate)
    gate_back = (acted_back * upper * sigma * (1.0 + gate * (1.0 - sigma))).astype(jnp.bfloat16)
    up_back = (acted_back * gate * sigma).astype(jnp.bfloat16)
    gate_grad = lead_dot(second, gate_back)
    up_grad = lead_dot(second, up_back)
    second_back = tail_dot(gate_back, gate_weight) + tail_dot(up_back, up_weight)
    _, norm_back = jax.vjp(norm_rows, hidden, second_gain.astype(jnp.float32))
    hidden_part, second_gain_grad = norm_back(second_back)
    hidden_back = cotangent + hidden_part
    hidden_bf = hidden_back.astype(jnp.bfloat16)
    output_grad = lead_dot(mixed_bf, hidden_bf)
    return (hidden_back, hidden_bf, (second_gain_grad, output_grad, gate_grad, up_grad, down_grad))

def backward_mixer(inputs, hidden_back, hidden_bf, saved, mats):
    normed, mixed_bf, mixer_back, hidden, second, gate, upper, acted = saved
    norm_gain, output_weight = (mats[0], mats[7])
    mixed_back = tail_dot(hidden_bf, output_weight)
    terms = mixer_back(mixed_back)
    normed_back = jnp.zeros(normed.shape, jnp.float32)
    weight_grads = []
    for index in range(6):
        rounded = terms[index].astype(jnp.bfloat16)
        weight_grads.append(lead_dot(normed, rounded))
        normed_back = normed_back + tail_dot(rounded, mats[1 + index])
    _, norm_back = jax.vjp(norm_rows, inputs, norm_gain.astype(jnp.float32))
    input_part, norm_gain_grad = norm_back(normed_back)
    inputs_grad = hidden_back + input_part
    return (inputs_grad, tuple([norm_gain_grad] + weight_grads), tuple(terms[6:]))

def layer_pass(inputs, cotangent, starts, filled, mats, smalls):
    masks = token_masks(starts, filled, smalls[0].shape[0])
    outputs, saved = forward(inputs, masks, mats, smalls)
    hidden_back, hidden_bf, late = backward_top(cotangent, saved, mats)
    inputs_grad, early, small = backward_mixer(inputs, hidden_back, hidden_bf, saved, mats)
    return (outputs, inputs_grad, late, early, small)

def reference(inputs, cotangent, starts, filled, norm_gain, query_weight, key_weight, value_weight, decay_weight, beta_weight, gating_weight, output_weight, second_gain, gate_weight, up_weight, down_weight, conv_query, conv_key, conv_value, decay_log, decay_bias, head_gain):
    mats = (norm_gain, query_weight, key_weight, value_weight, decay_weight, beta_weight, gating_weight, output_weight, second_gain, gate_weight, up_weight, down_weight)
    smalls = (conv_query, conv_key, conv_value, decay_log, decay_bias, head_gain)
    group = math.gcd(DEVICES, 8) * TOK_DEV
    count = TOKENS // group
    per_block = group // SPAN
    late_init = tuple((jnp.zeros(mats[index].shape, jnp.float32) for index in (8, 7, 9, 10, 11)))
    early_init = tuple((jnp.zeros(mats[index].shape, jnp.float32) for index in range(7)))
    small_init = tuple((jnp.zeros(piece.shape, jnp.float32) for piece in smalls))

    def visit(carry, block):
        rows, cots, begin, fill = block
        result, inputs_grad, late, early, small = layer_pass(rows, cots, begin, fill, mats, smalls)
        carry = jax.tree.map(jnp.add, carry, (late, early, small))
        return (carry, (result, inputs_grad))
    sums, (result, inputs_grad) = lax.scan(visit, (late_init, early_init, small_init), (inputs.reshape(count, group, D), cotangent.reshape(count, group, D), starts.reshape(count, per_block), filled.reshape(count, per_block)))
    late, early, small = sums
    return (result.reshape(TOKENS, D), inputs_grad.reshape(TOKENS, D), early[0], early[1], early[2], early[3], early[4], early[5], early[6], late[1], late[0], late[2], late[3], late[4], small[0], small[1], small[2], small[3], small[4], small[5])
```

```python
from functools import partial

import jax
import jax.numpy as jnp
from jax import lax
from jax.experimental import pallas as pl
from jax.experimental.pallas import tpu as pltpu
from jax.sharding import PartitionSpec as P

DK = 128
DV = 256
SPAN = 64


EPS = 1e-06
HIGH = lax.Precision.HIGH


def norm_rows(values, gain):
    return values * lax.rsqrt(jnp.mean(values * values, axis=-1, keepdims=True) + EPS) * gain


def unit_heads(values):
    return values * lax.rsqrt(jnp.sum(values * values, axis=-1, keepdims=True) + EPS)


def lead_dot(left, right):
    return lax.dot_general(
        left, right, (((0,), (0,)), ((), ())), preferred_element_type=jnp.float32
    )


def tail_dot(left, right):
    return lax.dot_general(
        left, right, (((1,), (1,)), ((), ())), preferred_element_type=jnp.float32
    )


def short_conv(values, taps, same):
    total = values * taps[0]
    for back in range(1, taps.shape[0]):
        moved = jnp.concatenate(
            [jnp.zeros((back, values.shape[1]), values.dtype), values[:-back]], axis=0
        )
        total = total + moved * taps[back] * same[back]
    return jax.nn.silu(total)


def token_masks(starts, filled, taps):
    count = starts.shape[0]
    place = jnp.arange(count, dtype=jnp.int32)
    upto = jnp.sum(jnp.where(place[:, None] >= place[None, :], starts[None, :], 0), axis=1)
    seq_ids = jnp.repeat(upto, SPAN)
    within = jnp.arange(count * SPAN, dtype=jnp.int32) % SPAN
    valid = (within < jnp.repeat(filled, SPAN)).astype(jnp.float32)[:, None]
    same = [jnp.ones_like(valid)]
    for back in range(1, taps):
        earlier = jnp.concatenate([jnp.full((back,), -1, jnp.int32), seq_ids[:-back]])
        same.append((earlier == seq_ids).astype(jnp.float32)[:, None])
    return (same, starts.astype(jnp.float32), valid)


def masked_product(equation, left, right):
    return jnp.einsum(equation, left, right, precision=HIGH)


def merge_inverse(strict_lower):
    size = strict_lower.shape[-1]
    rows = lax.broadcasted_iota(jnp.int32, (size, size), 0)
    cols = lax.broadcasted_iota(jnp.int32, (size, size), 1)
    pair = (rows // 2 == cols // 2).astype(strict_lower.dtype)
    inverse = jnp.eye(size, dtype=strict_lower.dtype) - strict_lower * pair
    width = 2
    while width < size:
        joint = (rows // (2 * width) == cols // (2 * width)) & (rows // width != cols // width)
        corner = strict_lower * joint.astype(strict_lower.dtype)
        corner = masked_product("nhij,nhjk->nhik", corner, inverse)
        inverse = inverse - masked_product("nhij,nhjk->nhik", inverse, corner)
        width *= 2
    return inverse


@jax.custom_vjp
def lower_inverse(strict_lower):
    return merge_inverse(strict_lower)


def lower_inverse_fwd(strict_lower):
    inverse = merge_inverse(strict_lower)
    return inverse, inverse


def lower_inverse_bwd(inverse, cot):
    part = masked_product("nhji,nhjk->nhik", inverse, cot)
    return (-masked_product("nhij,nhkj->nhik", part, inverse),)


lower_inverse.defvjp(lower_inverse_fwd, lower_inverse_bwd)


def run_chain(steps, adds):
    state = jnp.zeros(adds.shape[1:], adds.dtype)
    states = [state]
    for index in range(steps.shape[0] - 1):
        if index == 0:
            state = adds[0]
        else:
            state = masked_product("hij,hje->hie", steps[index], state) + adds[index]
        states.append(state)
    return jnp.stack(states)


@jax.custom_vjp
def chain(steps, adds):
    return run_chain(steps, adds)


def chain_fwd(steps, adds):
    states = run_chain(steps, adds)
    return states, (steps, states)


def chain_bwd(saved, cot):
    steps, states = saved
    last = steps.shape[0] - 1
    grads = [jnp.zeros(cot.shape[1:], cot.dtype)]
    grad = cot[last]
    for index in range(last - 1, -1, -1):
        grads.append(grad)
        if index:
            grad = cot[index] + masked_product("hij,hie->hje", steps[index], grad)
    adds_back = jnp.stack(grads[::-1])
    return masked_product("nhie,nhje->nhij", adds_back, states), adds_back


chain.defvjp(chain_fwd, chain_bwd)


def delta_rule(query, key, value, beta, decay, starts):
    count = starts.shape[0]

    def blocks(values):
        shaped = values.reshape((count, values.shape[0] // count) + values.shape[1:])
        return jnp.swapaxes(shaped, 1, 2)

    query, key, value = blocks(query), blocks(key), blocks(value)
    beta, decay = blocks(beta), blocks(decay)
    depth = key.shape[-1]
    size = decay.shape[-1]
    rows = lax.broadcasted_iota(jnp.int32, (size, size), 0)
    cols = lax.broadcasted_iota(jnp.int32, (size, size), 1)
    inside = rows >= cols
    lower = inside.astype(decay.dtype)
    strict = (rows > cols).astype(decay.dtype)
    total = jnp.einsum("nhj,ij->nhi", decay, lower, precision=lax.Precision.HIGHEST)
    spread = total[..., :, None] - total[..., None, :]
    factor = jnp.exp(jnp.where(inside, spread, 0.0)) * lower
    both = masked_product("nhid,nhjd->nhij", jnp.concatenate([key, query], axis=2), key)
    system = beta[..., None] * both[:, :, :size] * factor * strict
    scores = both[:, :, size:] * factor
    inverse = lower_inverse(system)
    growth = jnp.exp(total)[..., None]
    wanted = beta[..., None] * jnp.concatenate([growth * key, value], axis=3)
    solved = masked_product("nhij,nhje->nhie", inverse, wanted)
    final = total[..., -1:]
    carried = key * jnp.exp(final - total)[..., None]
    moved = masked_product("nhcd,nhce->nhde", carried, solved)
    keep = 1.0 - jnp.concatenate([starts[1:], jnp.ones_like(starts[:1])])
    keep = keep[:, None, None, None]
    identity = jnp.eye(depth, dtype=key.dtype)
    steps = keep * (jnp.exp(final)[..., None] * identity - moved[..., :depth])
    states = chain(steps, keep * moved[..., depth:])
    reads = jnp.concatenate([solved[..., :depth], growth * query], axis=2)
    read = masked_product("nhcd,nhde->nhce", reads, states)
    fresh = solved[..., depth:] - read[:, :, :size]
    result = read[:, :, size:] + masked_product("nhij,nhje->nhie", scores, fresh)
    return jnp.swapaxes(result, 1, 2).reshape(count * size, query.shape[1], value.shape[-1])


def mixer(
    same,
    starts,
    valid,
    query_pre,
    key_pre,
    value_pre,
    decay_pre,
    beta_pre,
    gating_pre,
    conv_query,
    conv_key,
    conv_value,
    decay_log,
    decay_bias,
    head_gain,
):
    count = query_pre.shape[0]
    local = query_pre.shape[1] // DK
    query = unit_heads(short_conv(query_pre, conv_query, same).reshape(count, local, DK)) * DK ** (
        -0.5
    )
    key = unit_heads(short_conv(key_pre, conv_key, same).reshape(count, local, DK))
    value = short_conv(value_pre, conv_value, same).reshape(count, local, DV)
    beta = jax.nn.sigmoid(beta_pre)
    decay = -jnp.exp(decay_log) * jax.nn.softplus(decay_pre + decay_bias)
    attended = delta_rule(query, key, value, beta, decay, starts)
    normal = (
        attended
        * lax.rsqrt(jnp.mean(attended * attended, axis=-1, keepdims=True) + EPS)
        * head_gain
    )
    gated = normal * jax.nn.silu(gating_pre.reshape(count, local, DV)) * valid[:, :, None]
    return gated.reshape(count, local * DV)


MESH = pl.DeviceIdType.MESH
LANES = 128
VMEM_BYTES = 52 * 2**20


def push(source, target, send, recv, peer):
    return pltpu.make_async_remote_copy(
        src_ref=source,
        dst_ref=target,
        send_sem=send,
        recv_sem=recv,
        device_id=peer,
        device_id_type=MESH,
    )


def row_peers(n_dp):
    dp, fsdp = lax.axis_index("dp"), lax.axis_index("fsdp")
    return [(lax.rem(dp + step, n_dp), fsdp) for step in range(1, n_dp)]


def head_peers(n_fsdp):
    dp, fsdp = lax.axis_index("dp"), lax.axis_index("fsdp")
    return [(dp, lax.rem(fsdp + step, n_fsdp)) for step in range(1, n_fsdp)]


def greet(peers):
    barrier = pltpu.get_barrier_semaphore()
    for peer in peers:
        pl.semaphore_signal(barrier, inc=1, device_id=peer, device_id_type=MESH)
    pl.semaphore_wait(barrier, len(peers))


def settle(copies):
    for copy in copies:
        copy.wait()


def gain_row(slots, which, width):
    n_dp = slots.shape[0]
    per_tile = max(1, n_dp * slots.shape[2] // width)
    tiles = []
    for first in range(0, n_dp, per_tile):
        tile = slots[first, which : which + 1, :]
        for more in range(first + 1, first + per_tile):
            tile = tile + slots[more, which : which + 1, :]
        tiles.append(tile)
    return jnp.concatenate(tiles, axis=1)


def scale_of(values):
    return lax.rsqrt(jnp.mean(values * values, axis=-1, keepdims=True) + EPS)


def norm_back(values, gain, cot):
    scale = scale_of(values)
    scaled = values * scale
    pulled = cot * gain
    back = scale * (pulled - scaled * jnp.mean(pulled * scaled, axis=-1, keepdims=True))
    return back, jnp.sum(cot * scaled, axis=0, keepdims=True)


def enter_kernel(
    n_dp, n_fsdp, inputs, gain, entry, normed_all, entry_all, gains,
    gain_send, gain_recv, entry_send, entry_recv, rows_send, rows_recv, local,
):
    dp, fsdp = lax.axis_index("dp"), lax.axis_index("fsdp")
    rows, depth = inputs.shape[0], entry.shape[0]
    along, across = row_peers(n_dp), head_peers(n_fsdp)
    greet(along + across)
    copies = []
    for index, peer in enumerate(along):
        copies.append(push(gain, gains.at[dp], gain_send.at[index], gain_recv.at[index], peer))
        copies[-1].start()
    heavy = []
    here = entry_all.at[pl.ds(dp * depth, depth)]
    for index, peer in enumerate(along):
        heavy.append(push(entry, here, entry_send.at[index], entry_recv.at[index], peer))
        heavy[-1].start()
    own = pltpu.make_async_copy(entry, here, local.at[0])
    own.start()
    gains[dp] = gain[...]
    scaled = inputs[...] * scale_of(inputs[...])
    settle(copies)
    mine = pl.ds(fsdp * rows, rows)
    normed_all[mine, :] = (scaled * gain_row(gains, 0, inputs.shape[1])).astype(jnp.bfloat16)
    for index, peer in enumerate(across):
        heavy.append(
            push(
                normed_all.at[mine], normed_all.at[mine], rows_send.at[index], rows_recv.at[index],
                peer,
            )
        )
        heavy[-1].start()
    own.wait()
    settle(heavy)


def reduce_rows(n_fsdp, terms, slots, send, recv):
    fsdp = lax.axis_index("fsdp")
    rows = terms.shape[0] // n_fsdp
    copies = []
    for index, peer in enumerate(head_peers(n_fsdp)):
        block = terms.at[pl.ds(pl.multiple_of(peer[1] * rows, rows), rows)]
        copies.append(push(block, slots.at[index], send.at[index], recv.at[index], peer))
        copies[-1].start()
    settle(copies)
    total = terms[pl.ds(pl.multiple_of(fsdp * rows, rows), rows), :].astype(jnp.float32)
    for index in range(n_fsdp - 1):
        total = total + slots[index].astype(jnp.float32)
    return total


def spread_rows(n_fsdp, rows_all, send, recv):
    fsdp = lax.axis_index("fsdp")
    rows = rows_all.shape[0] // n_fsdp
    mine = pl.ds(pl.multiple_of(fsdp * rows, rows), rows)
    copies = []
    for index, peer in enumerate(head_peers(n_fsdp)):
        copies.append(
            push(rows_all.at[mine], rows_all.at[mine], send.at[index], recv.at[index], peer)
        )
        copies[-1].start()
    settle(copies)


def hidden_kernel(
    n_fsdp, terms, inputs, gains, hidden, second_all,
    slots, sum_send, sum_recv, rows_send, rows_recv,
):
    fsdp = lax.axis_index("fsdp")
    rows = inputs.shape[0]
    greet(head_peers(n_fsdp))
    value = inputs[...] + reduce_rows(n_fsdp, terms, slots, sum_send, sum_recv)
    hidden[...] = value
    mine = pl.ds(pl.multiple_of(fsdp * rows, rows), rows)
    second_all[mine, :] = (value * scale_of(value) * gain_row(gains, 1, hidden.shape[1])).astype(jnp.bfloat16)
    spread_rows(n_fsdp, second_all, rows_send, rows_recv)


def turn_kernel(
    n_fsdp, terms, hidden, cotangent, gains, hidden_back, hidden_all, gain_grad,
    slots, sum_send, sum_recv, rows_send, rows_recv,
):
    fsdp = lax.axis_index("fsdp")
    rows = hidden.shape[0]
    greet(head_peers(n_fsdp))
    cot = reduce_rows(n_fsdp, terms, slots, sum_send, sum_recv)
    back, grad = norm_back(hidden[...], gain_row(gains, 1, hidden.shape[1]), cot)
    back = back + cotangent[...]
    hidden_back[...] = back
    gain_grad[...] = grad
    mine = pl.ds(pl.multiple_of(fsdp * rows, rows), rows)
    hidden_all[mine, :] = back.astype(jnp.bfloat16)
    spread_rows(n_fsdp, hidden_all, rows_send, rows_recv)


def leave_kernel(
    n_dp, n_fsdp, terms, inputs, hidden_back, gains, early, small, inputs_grad, early_sum,
    small_sum, slots, early_slots, small_slots, shared_slots,
    sum_send, sum_recv, early_send, early_recv, small_send, small_recv, shared_send, shared_recv,
):
    dp, fsdp = lax.axis_index("dp"), lax.axis_index("fsdp")
    along, across = row_peers(n_dp), head_peers(n_fsdp)
    depth = early.shape[0] // n_dp
    greet(along + across)
    heavy = []
    for index, peer in enumerate(along):
        block = early.at[pl.ds(pl.multiple_of(peer[0] * depth, depth), depth)]
        heavy.append(
            push(block, early_slots.at[index], early_send.at[index], early_recv.at[index], peer)
        )
        heavy[-1].start()
    cot = reduce_rows(n_fsdp, terms, slots, sum_send, sum_recv)
    back, grad = norm_back(inputs[...], gain_row(gains, 0, inputs.shape[1]), cot)
    inputs_grad[...] = hidden_back[...] + back
    count = grad.shape[1] // LANES
    base = small.shape[0] - count
    small_slots[dp] = small[...]
    for index in range(count):
        small_slots[dp, base + index : base + index + 1, :] = grad[
            :, index * LANES : (index + 1) * LANES
        ]
    copies = []
    for index, peer in enumerate(along):
        copies.append(
            push(
                small_slots.at[dp], small_slots.at[dp], small_send.at[index], small_recv.at[index],
                peer,
            )
        )
        copies[-1].start()
    settle(copies)
    total = small_slots[0]
    for index in range(1, n_dp):
        total = total + small_slots[index]
    alone = shared_slots.shape[1]
    skip = small.shape[0] - alone
    small_sum[0:skip, :] = total[0:skip, :]
    shared_slots[fsdp] = total[skip:, :]
    copies = []
    for index, peer in enumerate(across):
        copies.append(
            push(
                shared_slots.at[fsdp], shared_slots.at[fsdp], shared_send.at[index],
                shared_recv.at[index], peer,
            )
        )
        copies[-1].start()
    settle(copies)
    total = shared_slots[0]
    for index in range(1, n_fsdp):
        total = total + shared_slots[index]
    small_sum[skip:, :] = total
    settle(heavy)
    total = early[pl.ds(pl.multiple_of(dp * depth, depth), depth), :].astype(jnp.float32)
    for index in range(n_dp - 1):
        total = total + early_slots[index].astype(jnp.float32)
    early_sum[...] = total


def pairs(*counts):
    made = []
    for count in counts:
        made += [pltpu.SemaphoreType.DMA((count,)), pltpu.SemaphoreType.DMA((count,))]
    return made


def comm_call(kernel, shapes, scratch, number, *args):
    whole = pl.BlockSpec(memory_space=pltpu.VMEM)
    return pl.pallas_call(
        kernel,
        out_shape=[jax.ShapeDtypeStruct(shape, kind) for shape, kind in shapes],
        in_specs=[whole] * len(args),
        out_specs=[whole] * len(shapes),
        scratch_shapes=scratch,
        compiler_params=pltpu.CompilerParams(
            collective_id=number, has_side_effects=True, vmem_limit_bytes=VMEM_BYTES
        ),
    )(*args)


def on_device(
    n_dp,
    n_fsdp,
    inputs,
    cotangent,
    starts,
    filled,
    norm_gain,
    query_weight,
    key_weight,
    value_weight,
    decay_weight,
    beta_weight,
    gating_weight,
    output_weight,
    second_gain,
    gate_weight,
    up_weight,
    down_weight,
    conv_query,
    conv_key,
    conv_value,
    decay_log,
    decay_bias,
    head_gain,
):
    f32, bf16 = jnp.float32, jnp.bfloat16
    rows, width = inputs.shape
    all_rows = rows * n_fsdp
    widths = [
        query_weight.shape[1],
        key_weight.shape[1],
        value_weight.shape[1],
        gating_weight.shape[1],
        decay_weight.shape[1],
        beta_weight.shape[1],
    ]
    ends = [sum(widths[: index + 1]) for index in range(6)]
    bounds = list(zip([0] + ends[:-1], ends))
    spare = -ends[-1] % LANES
    packed = jnp.concatenate(
        [
            query_weight,
            key_weight,
            value_weight,
            gating_weight,
            decay_weight,
            beta_weight,
            jnp.zeros((query_weight.shape[0], spare), bf16),
        ],
        axis=1,
    )
    part = norm_gain.shape[0]
    gain_block = lax.dynamic_update_slice(
        jnp.zeros((8, max(LANES, part)), f32),
        jnp.stack([norm_gain, second_gain]).astype(f32),
        (0, lax.rem(lax.axis_index("dp") * part, LANES) if part < LANES else 0),
    )
    local_out = output_weight.T
    local_feed = jnp.stack([gate_weight, up_weight, down_weight.T])
    out_t = lax.all_gather(local_out, "dp", axis=0, tiled=True)
    feed = lax.all_gather(local_feed, "dp", axis=1, tiled=True)
    cot_all = lax.all_gather(cotangent.astype(bf16), "fsdp", axis=0, tiled=True)
    same, starts_f, valid = token_masks(starts, filled, conv_query.shape[0])
    normed_all, entry, gains = comm_call(
        partial(enter_kernel, n_dp, n_fsdp),
        [
            ((all_rows, width), bf16),
            ((packed.shape[0] * n_dp, packed.shape[1]), bf16),
            ((n_dp,) + gain_block.shape, f32),
        ],
        pairs(n_dp - 1, n_dp - 1, n_fsdp - 1) + [pltpu.SemaphoreType.DMA((1,))],
        0,
        inputs,
        gain_block,
        packed,
    )
    projected = jnp.dot(normed_all, entry, preferred_element_type=f32)
    pres = [projected[:, low:high] for low, high in bounds]
    mixed, mixer_back = jax.vjp(
        partial(mixer, same, starts_f, valid),
        pres[0],
        pres[1],
        pres[2],
        pres[4],
        pres[5],
        pres[3],
        conv_query,
        conv_key,
        conv_value,
        decay_log,
        decay_bias,
        head_gain,
    )
    mixed_bf = mixed.astype(bf16)
    slots = pltpu.VMEM((n_fsdp - 1, rows, width), bf16)
    hidden, second_all = comm_call(
        partial(hidden_kernel, n_fsdp),
        [((rows, width), f32), ((all_rows, width), bf16)],
        [slots] + pairs(n_fsdp - 1, n_fsdp - 1),
        1,
        tail_dot(mixed_bf, out_t).astype(bf16),
        inputs,
        gains,
    )
    gate = jnp.dot(second_all, feed[0], preferred_element_type=f32)
    upper = jnp.dot(second_all, feed[1], preferred_element_type=f32)
    sigma = jax.nn.sigmoid(gate)
    acted = (gate * sigma * upper).astype(bf16)
    acted_back = jnp.dot(cot_all, feed[2], preferred_element_type=f32)
    gate_back = (acted_back * upper * sigma * (1.0 + gate * (1.0 - sigma))).astype(bf16)
    up_back = (acted_back * gate * sigma).astype(bf16)
    hidden_back, hidden_all, second_gain_grad = comm_call(
        partial(turn_kernel, n_fsdp),
        [((rows, width), f32), ((all_rows, width), bf16), ((1, width), f32)],
        [slots] + pairs(n_fsdp - 1, n_fsdp - 1),
        2,
        (tail_dot(gate_back, feed[0]) + tail_dot(up_back, feed[1])).astype(bf16),
        hidden,
        cotangent,
        gains,
    )
    hidden_all, late_rows, late_cols, late_acted, late_gate, late_up = lax.optimization_barrier(
        (hidden_all, second_all, cot_all, acted, gate_back, up_back)
    )
    late = jnp.stack(
        [
            lead_dot(late_rows, late_gate).astype(bf16),
            lead_dot(late_rows, late_up).astype(bf16),
            lead_dot(late_cols, late_acted).astype(bf16),
        ]
    )
    late_sums = lax.psum_scatter(late, "dp", scatter_dimension=1, tiled=True)
    late_sums = late_sums.astype(f32)
    outputs = hidden + lax.psum_scatter(
        tail_dot(late_acted, feed[2]).astype(bf16), "fsdp", scatter_dimension=0, tiled=True
    ).astype(f32)
    mixed_back = jnp.dot(hidden_all, out_t, preferred_element_type=f32)
    terms = mixer_back(mixed_back)
    order = [0, 1, 2, 5, 3, 4]
    rounded = jnp.concatenate(
        [terms[index].astype(bf16) for index in order] + [jnp.zeros((all_rows, spare), bf16)],
        axis=1,
    )
    early = jnp.concatenate(
        [
            lead_dot(hidden_all, mixed_bf).astype(bf16),
            lead_dot(normed_all, rounded).astype(bf16),
        ],
        axis=1,
    )
    singles = jnp.concatenate([terms[9], terms[10]])
    small = jnp.concatenate(
        [
            terms[6].reshape(-1, LANES),
            terms[7].reshape(-1, LANES),
            terms[8].reshape(-1, LANES),
            jnp.pad(singles, (0, -singles.shape[0] % LANES)).reshape(-1, LANES),
        ],
        axis=0,
    )
    lone = -(-small.shape[0] // 8) * 8
    small = jnp.pad(small, ((0, lone - small.shape[0]), (0, 0)))
    shared = jnp.concatenate(
        [
            jnp.pad(terms[11].reshape(-1, LANES), ((0, -terms[11].shape[0] // LANES % 8), (0, 0))),
            second_gain_grad.reshape(-1, LANES),
            jnp.zeros((width // LANES, LANES), f32),
        ],
        axis=0,
    )
    small = jnp.concatenate([small, shared], axis=0)
    inputs_grad, early_sums, sums = comm_call(
        partial(leave_kernel, n_dp, n_fsdp),
        [
            ((rows, width), f32),
            ((early.shape[0] // n_dp, early.shape[1]), f32),
            (small.shape, f32),
        ],
        [
            slots,
            pltpu.VMEM((n_dp - 1, early.shape[0] // n_dp, early.shape[1]), bf16),
            pltpu.VMEM((n_dp,) + small.shape, f32),
            pltpu.VMEM((n_fsdp,) + shared.shape, f32),
        ]
        + pairs(n_fsdp - 1, n_dp - 1, n_dp - 1, n_fsdp - 1),
        3,
        tail_dot(rounded, entry).astype(bf16),
        inputs,
        hidden_back,
        gains,
        early,
        small,
    )
    out_width = mixed_bf.shape[1]
    output_sum = early_sums[:, :out_width].T
    entry_sums = early_sums[:, out_width:]
    parts = [entry_sums[:, low:high] for low, high in bounds]
    taken, pieces = 0, []
    for index in (6, 7, 8):
        count = terms[index].size // LANES
        pieces.append(sums[taken : taken + count].reshape(terms[index].shape))
        taken += count
    locals_ = terms[9].shape[0]
    singles = sums[taken:lone].reshape(-1)
    tiles = width // LANES
    return (
        outputs,
        inputs_grad,
        sums[-tiles:].reshape(-1),
        parts[0],
        parts[1],
        parts[2],
        parts[4],
        parts[5],
        parts[3],
        output_sum,
        sums[-2 * tiles : -tiles].reshape(-1),
        late_sums[0],
        late_sums[1],
        late_sums[2].T,
        pieces[0],
        pieces[1],
        pieces[2],
        singles[:locals_],
        singles[locals_ : 2 * locals_],
        sums[lone : lone + head_gain.shape[0] // LANES].reshape(-1),
    )


def solution(mesh):
    in_specs = (
        P(("dp", "fsdp"), None),
        P(("dp", "fsdp"), None),
        P("dp"),
        P("dp"),
        P("dp"),
        P("dp", "fsdp"),
        P("dp", "fsdp"),
        P("dp", "fsdp"),
        P("dp", "fsdp"),
        P("dp", "fsdp"),
        P("dp", "fsdp"),
        P("fsdp", "dp"),
        P("dp"),
        P("dp", "fsdp"),
        P("dp", "fsdp"),
        P("fsdp", "dp"),
        P(None, "fsdp"),
        P(None, "fsdp"),
        P(None, "fsdp"),
        P("fsdp"),
        P("fsdp"),
        P(),
    )
    out_specs = (
        P(("dp", "fsdp"), None),
        P(("dp", "fsdp"), None),
        P(),
        P("dp", "fsdp"),
        P("dp", "fsdp"),
        P("dp", "fsdp"),
        P("dp", "fsdp"),
        P("dp", "fsdp"),
        P("dp", "fsdp"),
        P("fsdp", "dp"),
        P(),
        P("dp", "fsdp"),
        P("dp", "fsdp"),
        P("fsdp", "dp"),
        P(None, "fsdp"),
        P(None, "fsdp"),
        P(None, "fsdp"),
        P("fsdp"),
        P("fsdp"),
        P(),
    )
    return jax.shard_map(
        partial(on_device, mesh.shape["dp"], mesh.shape["fsdp"]), mesh=mesh, in_specs=in_specs, out_specs=out_specs, check_vma=False
    )
```
